32 devices in a mesh: layer: 2 (over core), prow: 4 (over z), pcol: 4 (over y, x).
Axes of the slice: x: 2, y: 2, z: 4, core: 2. Of those that a mesh axis runs over, the one named last changes fastest.
Arguments:
- factor: bfloat16 [2, 4, 4, 4, 4, 256, 256], P('layer', 'prow', None, None, 'pcol'), may hold values from -0.1875 to 0.1875
- factor_scale: float32 [2, 4, 4, 4, 4], P('layer', 'prow', None, None, 'pcol'), may hold values from 0.25 to 4
- sub_pattern: int32 [2, 4, 4, 4, 4], P('layer', 'prow', None, None, 'pcol'), may hold values from 0 to 1, as said below
- coupling: bfloat16 [2, 4, 4, 4, 4, 256, 256], P('layer', 'prow', None, None, 'pcol'), may hold values from -0.1875 to 0.1875
- coupling_scale: float32 [2, 4, 4, 4, 4], P('layer', 'prow', None, None, 'pcol'), may hold values from 0.25 to 4
- top_pattern: int32 [2, 4, 4, 4, 4], P('layer', 'prow', None, None, 'pcol'), may hold values 0 or 1
- diag_inverse: float32 [2, 4, 4, 256, 256], P('layer', 'prow', 'pcol'), may hold values from -1 to 2
- top_inverse: float32 [4, 4, 256, 256], P('prow', 'pcol'), may hold values from -1 to 2
- rhs_sub: float32 [2, 4, 4, 256, 256], P('layer', 'prow', 'pcol'), may hold values from -6 to 6
- rhs_top: float32 [4, 4, 256, 256], P('prow', 'pcol'), may hold values from -6 to 6
Outputs:
- sol_sub: float32 [2, 4, 4, 256, 256], P('layer', 'prow', 'pcol')
- sol_top: float32 [4, 4, 256, 256], P('prow', 'pcol')
The draws below stay inside these ranges and needn't reach their ends.
Inputs may be any that keep to these rules, and one draw needn't show every extreme that they name: The supernodes of each layer fall into 3 levels; sub_pattern is 1 only where the column supernode's level is below the row supernode's level.
All inputs are finite; a program needn't handle non-finite values. No bound on the sum of `top_pattern` on one device may be relied on, other than what follows from the above.
Results may differ from the reference program's by a relative error of at most 0.02.
Values may be sent and summed in bfloat16 or wider, within the bound.
No kernel may reach another device: no remote copies, remote signals or barrier semaphores. Data moves between devices by JAX's collectives and lax.ppermute only.
A program may use at most 64 MiB of HBM per device.

```python
import math
import jax
import jax.numpy as jnp
from jax import lax

W = 256
R = 256
LEVELS = 3
LAYERS = 2
GRID_ROWS = 4
GRID_COLS = 4


def lower_inverse(key, leading):
    key_off, key_diag = jax.random.split(key)
    full_shape = leading + (W, W)
    spread = jax.random.normal(key_off, full_shape, jnp.float32)
    diagonal = jax.random.uniform(key_diag, leading + (W,), jnp.float32, 0.6, 1.4)
    row_index = lax.broadcasted_iota(jnp.int32, (W, W), 0)
    col_index = lax.broadcasted_iota(jnp.int32, (W, W), 1)
    strict = (row_index > col_index).astype(jnp.float32)
    identity = (row_index == col_index).astype(jnp.float32)
    return spread * strict * (0.6 / math.sqrt(W)) + diagonal[..., :, None] * identity


def draw_diag_inverse(key, part):
    return lower_inverse(jax.random.fold_in(key, 21), (LAYERS, GRID_ROWS, GRID_COLS))


def draw_top_inverse(key, part):
    return lower_inverse(jax.random.fold_in(key, 22), (GRID_ROWS, GRID_COLS))


def draw_sub_pattern(key, part):
    count = GRID_ROWS * GRID_COLS
    layer_keys = jax.random.split(jax.random.fold_in(key, 11), LAYERS)
    order = jax.vmap(lambda single_key: jax.random.permutation(single_key, count))(layer_keys)
    rank_level = jnp.zeros((LAYERS, count), jnp.int32)
    for step_index in range(1, LEVELS):
        rank_level = rank_level + (order >= count - count // 2 ** step_index).astype(jnp.int32)
    coins = jax.random.randint(jax.random.fold_in(key, 12), (LAYERS, count, count), 0, 2)
    below = (rank_level[:, None, :] < rank_level[:, :, None]).astype(jnp.int32)
    return (below * coins).reshape(LAYERS, GRID_ROWS, GRID_COLS, GRID_ROWS, GRID_COLS)


def with_ends(values, own_key, low, top_value):
    extent = values.shape
    index_at = [jax.random.randint(jax.random.fold_in(own_key, axis), (), 0, extent[axis]) for axis in range(len(extent))]
    values = values.at[tuple(index_at)].set(low)
    longest = extent.index(max(extent))
    index_at[longest] = (index_at[longest] + 1) % extent[longest]
    return values.at[tuple(index_at)].set(top_value)


def raised(array, rng, source, target, shards_of, factor):
    owner, partner = [(jnp.arange(array.shape[axis_at]) // (array.shape[axis_at] // shards_of)).reshape([-1 if axis == axis_at else 1 for axis in range(array.ndim)]) for axis_at in (source, target)]
    chosen = jax.random.permutation(rng, shards_of)[partner]
    strong = (owner == chosen) | (owner == (partner + shards_of // 2) % shards_of)
    return jnp.where(strong, factor * array, array)


def level_of(rng, dims, cuts, low, top_value):
    level = 1.0
    for position, shards_of in cuts:
        steps = jax.random.uniform(jax.random.fold_in(jax.random.fold_in(rng, 6), position), (shards_of,), jnp.float32, low / len(cuts), top_value / len(cuts))
        level = level * jnp.repeat(jnp.exp(steps), dims[position] // shards_of).reshape((-1,) + (1,) * (len(dims) - 1 - position))
    return level


def gaussian(own_key, extent, scale, limit, cuts=(), kind=jnp.bfloat16):
    level = level_of(own_key, extent, cuts, -0.22, 0.18) if cuts else 1.0
    values = jax.random.normal(own_key, extent, jnp.float32) * scale * level
    return jnp.minimum(jnp.maximum(values, -limit), limit).astype(kind)


def gaussian_with(key, extent, scale, bound, shards, heavy, kind=jnp.bfloat16):
    result = scale * jax.random.normal(key, extent, jnp.float32)
    if shards:
        result = result * level_of(key, extent, shards, -0.22, 0.18)
    return jnp.clip(raised(result, jax.random.fold_in(key, 3), *heavy), -bound, bound).astype(kind)


def setup_inputs(seed: int = 0) -> dict:
    splits = jax.random.split(jax.random.key(seed), 11)
    factor = gaussian_with(splits[0], (LAYERS, GRID_ROWS, GRID_COLS, GRID_ROWS, GRID_COLS, W, W), (W * GRID_ROWS * GRID_COLS // 2) ** -0.5, 0.1875, ((0, 2), (1, 4), (4, 4)), (4, 2, 4, 2.0))
    factor_scale = jnp.clip(jnp.exp(math.log(4.0) - 2.7725887 * jax.random.uniform(splits[1], (LAYERS, GRID_ROWS, GRID_COLS, GRID_ROWS, GRID_COLS), jnp.float32) ** level_of(splits[1], (LAYERS, GRID_ROWS, GRID_COLS, GRID_ROWS, GRID_COLS), ((0, 2), (1, 4), (4, 4)), -0.2, 0.2)), 0.25, 4.0)
    sub_pattern = draw_sub_pattern(jax.random.fold_in(splits[10], 71), 0)
    coupling = gaussian_with(splits[3], (LAYERS, GRID_ROWS, GRID_COLS, GRID_ROWS, GRID_COLS, W, W), (W * GRID_ROWS * GRID_COLS // 2) ** -0.5, 0.1875, ((0, 2), (1, 4), (4, 4)), (1, 3, 4, 2.0))
    coupling_scale = jnp.clip(jnp.exp(math.log(4.0) - 2.7725887 * jax.random.uniform(splits[4], (LAYERS, GRID_ROWS, GRID_COLS, GRID_ROWS, GRID_COLS), jnp.float32) ** level_of(splits[4], (LAYERS, GRID_ROWS, GRID_COLS, GRID_ROWS, GRID_COLS), ((0, 2), (1, 4), (4, 4)), -0.2, 0.2)), 0.25, 4.0)
    top_pattern = with_ends((jax.random.randint(splits[5], (LAYERS, GRID_ROWS, GRID_COLS, GRID_ROWS, GRID_COLS), 0, 2) < 1).astype(jnp.int32), jax.random.fold_in(splits[5], 1), 0, 1)
    diag_inverse = draw_diag_inverse(jax.random.fold_in(splits[10], 71), 0)
    top_inverse = draw_top_inverse(jax.random.fold_in(splits[10], 71), 0)
    rhs_sub = gaussian(splits[8], (LAYERS, GRID_ROWS, GRID_COLS, W, R), 1.0, 6.0, ((0, 2), (1, 4), (2, 4)), jnp.float32)
    rhs_top = gaussian(splits[9], (GRID_ROWS, GRID_COLS, W, R), 1.0, 6.0, ((0, 4), (1, 4)), jnp.float32)
    return {"factor": factor, "factor_scale": factor_scale, "sub_pattern": sub_pattern, "coupling": coupling, "coupling_scale": coupling_scale, "top_pattern": top_pattern, "diag_inverse": diag_inverse, "top_inverse": top_inverse, "rhs_sub": rhs_sub, "rhs_top": rhs_top}


HIGH_PREC = lax.Precision.HIGHEST


def apply_left(matrix, values):
    return jnp.einsum('...wk,...kr->...wr', matrix, values, precision=HIGH_PREC)


def apply_trans(matrix, values):
    return jnp.einsum('...kw,...kr->...wr', matrix, values, precision=HIGH_PREC)


def rounded_copy(values):
    return lax.optimization_barrier(values.astype(jnp.bfloat16)).astype(jnp.float32)


def forward_sum(blocks, scaling, values):
    grid_rows, grid_cols = values.shape[0], values.shape[1]
    shared = rounded_copy(values)
    flat_blocks = blocks.reshape((grid_rows * grid_cols,) + blocks.shape[2:])
    flat_scale = scaling.reshape((grid_rows * grid_cols,) + scaling.shape[2:])

    def one_row(paired):
        row_blocks, row_scale = paired
        terms = jnp.einsum('acwk,ackr->acwr', row_blocks.astype(jnp.float32), shared, precision=HIGH_PREC)
        terms = terms * row_scale[:, :, None, None]
        partial_value = rounded_copy(jnp.sum(terms, axis=0))
        return jnp.sum(partial_value, axis=0)

    sums = lax.map(one_row, (flat_blocks, flat_scale))
    return sums.reshape(values.shape)


def backward_sum(blocks, scaling, values):
    grid_rows, grid_cols = values.shape[0], values.shape[1]
    shared = rounded_copy(values)
    col_blocks = jnp.transpose(blocks, (2, 3, 0, 1, 4, 5)).reshape((grid_rows * grid_cols,) + (grid_rows, grid_cols) + blocks.shape[4:])
    col_scale = jnp.transpose(scaling, (2, 3, 0, 1)).reshape(grid_rows * grid_cols, grid_rows, grid_cols)

    def one_column(paired):
        these_blocks, these_scale = paired
        terms = jnp.einsum('pqkw,pqkr->pqwr', these_blocks.astype(jnp.float32), shared, precision=HIGH_PREC)
        terms = terms * these_scale[:, :, None, None]
        partial_value = rounded_copy(jnp.sum(terms, axis=1))
        return jnp.sum(partial_value, axis=0)

    sums = lax.map(one_column, (col_blocks, col_scale))
    return sums.reshape(values.shape)


def reference(factor, factor_scale, sub_pattern, coupling, coupling_scale, top_pattern, diag_inverse, top_inverse, rhs_sub, rhs_top):
    sub_weight = factor_scale * sub_pattern.astype(jnp.float32)
    top_weight = coupling_scale * top_pattern.astype(jnp.float32)
    forward_fields = []
    merged = jnp.zeros(rhs_top.shape, jnp.float32)
    for layer_index in range(LAYERS):
        solved = apply_left(diag_inverse[layer_index], rhs_sub[layer_index])
        for sweep_index in range(LEVELS - 1):
            lower_sum = forward_sum(factor[layer_index], sub_weight[layer_index], solved)
            solved = apply_left(diag_inverse[layer_index], rhs_sub[layer_index] - lower_sum)
        forward_fields.append(solved)
        merged = merged + forward_sum(coupling[layer_index], top_weight[layer_index], solved)
    top_fwd = apply_left(top_inverse, rhs_top - merged)
    sol_top = apply_trans(top_inverse, top_fwd)
    answers = []
    for layer_index in range(LAYERS):
        coupled = backward_sum(coupling[layer_index], top_weight[layer_index], sol_top)
        answer = apply_trans(diag_inverse[layer_index], forward_fields[layer_index] - coupled)
        for sweep_index in range(LEVELS - 1):
            upper_sum = backward_sum(factor[layer_index], sub_weight[layer_index], answer)
            answer = apply_trans(diag_inverse[layer_index], forward_fields[layer_index] - coupled - upper_sum)
        answers.append(answer)
    return jnp.stack(answers), sol_top
```

```python
import functools

import jax
import jax.numpy as jnp
from jax import lax
from jax.experimental import pallas as pl
from jax.experimental.pallas import tpu as pltpu
from jax.sharding import PartitionSpec as P

LEVELS = 3
CHUNKS = 2
HIGH_PREC = lax.Precision.HIGHEST
ROWS_FIRST = ((1,), (0,))
F32 = jnp.float32
BF16 = jnp.bfloat16

SMEM = pl.BlockSpec(memory_space=pltpu.SMEM)
VMEM = pl.BlockSpec(memory_space=pltpu.VMEM)


def partner(index, step, count):
    if count & (count - 1) == 0:
        return index ^ step
    return (index + step) % count


def source(index, step, count):
    if count & (count - 1) == 0:
        return index ^ step
    return (index + count - step) % count


def exchange(values, axis, count):
    received = [None] * count
    received[0] = values[0]
    for step in reversed(range(1, count)):
        pairs = [(index, partner(index, step, count)) for index in range(count)]
        received[step] = lax.ppermute(values[step], axis, pairs)
    return received


def spread(value, axis, count):
    return exchange([value] * count, axis, count)


def call(body, outs, specs, operands, name, flops):
    size = sum(x.size * x.dtype.itemsize for x in operands)
    return pl.pallas_call(
        body,
        out_shape=[jax.ShapeDtypeStruct(shape, dtype) for shape, dtype in outs],
        in_specs=specs,
        out_specs=[VMEM] * len(outs),
        name=name,
        cost_estimate=pl.CostEstimate(flops=flops, bytes_accessed=size, transcendentals=0),
        compiler_params=pltpu.CompilerParams(vmem_limit_bytes=16 * 1024 * 1024),
    )(*operands)


def solve_dot(a, b):
    return jnp.dot(a, b, precision=HIGH_PREC, preferred_element_type=F32)


def total_of(refs):
    total = refs[0][...].astype(F32)
    for ref in refs[1:]:
        total = total + ref[...].astype(F32)
    return total


def forward_products(blocks, weights, fields, rows, cols):
    size, width = fields[0].shape

    def body(weight_ref, blocks_ref, *refs):
        ins, outs = refs[:rows], refs[rows:]
        here_row, here_col = lax.axis_index("prow"), lax.axis_index("pcol")
        for step in range(cols):
            q = partner(here_col, step, cols)
            total = None
            for back in range(rows):
                a = source(here_row, back, rows)
                term = jnp.dot(blocks_ref[q * rows + a], ins[back][...], preferred_element_type=F32)
                term = term * weight_ref[q * rows + a]
                total = term if total is None else total + term
            outs[step][...] = total.astype(BF16)

    return call(
        body,
        [((size, width), BF16)] * cols,
        [SMEM, VMEM] + [VMEM] * rows,
        [weights, blocks] + list(fields),
        "forward_products",
        2 * rows * cols * size * size * width,
    )


def backward_products(blocks, weights, fields, rows, cols):
    width, size = fields[0].shape

    def body(weight_ref, blocks_ref, *refs):
        ins, outs = refs[:cols], refs[cols:]
        here_row, here_col = lax.axis_index("prow"), lax.axis_index("pcol")
        for step in range(rows):
            a = partner(here_row, step, rows)
            total = None
            for back in range(cols):
                q = source(here_col, back, cols)
                term = jnp.dot(ins[back][...], blocks_ref[q * rows + a], preferred_element_type=F32)
                term = term * weight_ref[q * rows + a]
                total = term if total is None else total + term
            outs[step][...] = total.astype(BF16)

    return call(
        body,
        [((width, size), BF16)] * rows,
        [SMEM, VMEM] + [VMEM] * cols,
        [weights, blocks] + list(fields),
        "backward_products",
        2 * rows * cols * size * size * width,
    )


def shards(
    factor,
    factor_scale,
    sub_pattern,
    coupling,
    coupling_scale,
    top_pattern,
    diag_inverse,
    top_inverse,
    rhs_sub,
    rhs_top,
):
    size = factor.shape[5]
    cols = factor.shape[2]
    rows = factor.shape[3]
    layers = lax.axis_size("layer")
    width = rhs_sub.shape[-1]
    chunk = width // CHUNKS
    blocks = factor.reshape(rows * cols, size, size)
    links = coupling.reshape(rows * cols, size, size)
    weights = (factor_scale * sub_pattern.astype(F32)).reshape(rows * cols)
    link_weights = (coupling_scale * top_pattern.astype(F32)).reshape(rows * cols)
    inverse = diag_inverse.reshape(size, size)
    top_matrix = top_inverse.reshape(size, size)
    own_rhs = rhs_sub.reshape(size, width)
    top_rhs = rhs_top.reshape(size, width)
    solve_flops = 12 * size * size * chunk

    def window(index):
        return slice(index * chunk, (index + 1) * chunk)

    def begin(index):
        def body(inv_ref, rhs_ref, out_ref):
            out_ref[...] = solve_dot(inv_ref[...], rhs_ref[:, window(index)]).astype(BF16)

        return call(body, [((size, chunk), BF16)], [VMEM] * 2, [inverse, own_rhs], "begin", solve_flops)[0]

    def forward_solve(index, parts):
        def body(inv_ref, rhs_ref, *refs):
            lower = total_of(refs[:-1])
            refs[-1][...] = solve_dot(inv_ref[...], rhs_ref[:, window(index)] - lower).astype(BF16)

        return call(
            body,
            [((size, chunk), BF16)],
            [VMEM] * (2 + cols),
            [inverse, own_rhs] + list(parts),
            "forward_solve",
            solve_flops,
        )[0]

    def forward_last(index, parts):
        def body(inv_ref, rhs_ref, *refs):
            lower = total_of(refs[:-2])
            solved = solve_dot(inv_ref[...], rhs_ref[:, window(index)] - lower)
            refs[-2][...] = solved.astype(BF16)
            refs[-1][...] = solved.T

        return call(
            body,
            [((size, chunk), BF16), ((chunk, size), F32)],
            [VMEM] * (2 + cols),
            [inverse, own_rhs] + list(parts),
            "forward_last",
            solve_flops,
        )

    def top_sum(parts):
        def body(*refs):
            refs[-1][...] = total_of(refs[:-1])

        return call(body, [((size, chunk), F32)], [VMEM] * cols, list(parts), "top_sum", size * chunk)[0]

    def top_solve(index, sums):
        def body(top_ref, rhs_ref, *refs):
            merged = total_of(refs[:-2])
            half = solve_dot(top_ref[...], rhs_ref[:, window(index)] - merged)
            answer_t = solve_dot(half.T, top_ref[...])
            refs[-2][...] = answer_t.T
            refs[-1][...] = answer_t.astype(BF16)

        return call(
            body,
            [((size, chunk), F32), ((chunk, size), BF16)],
            [VMEM] * (2 + layers),
            [top_matrix, top_rhs] + list(sums),
            "top_solve",
            2 * solve_flops,
        )

    def backward_first(solved_t, parts):
        def body(inv_ref, solved_ref, *refs):
            known = solved_ref[...] - total_of(refs[:-2])
            refs[-2][...] = known
            refs[-1][...] = solve_dot(known, inv_ref[...]).astype(BF16)

        return call(
            body,
            [((chunk, size), F32), ((chunk, size), BF16)],
            [VMEM] * (2 + rows),
            [inverse, solved_t] + list(parts),
            "backward_first",
            solve_flops,
        )

    def backward_solve(known, parts):
        def body(inv_ref, known_ref, *refs):
            upper = total_of(refs[:-1])
            refs[-1][...] = solve_dot(known_ref[...] - upper, inv_ref[...]).astype(BF16)

        return call(
            body,
            [((chunk, size), BF16)],
            [VMEM] * (2 + rows),
            [inverse, known] + list(parts),
            "backward_solve",
            solve_flops,
        )[0]

    def backward_last(known, parts):
        def body(inv_ref, known_ref, *refs):
            upper = total_of(refs[:-1])
            refs[-1][...] = solve_dot(known_ref[...] - upper, inv_ref[...]).T

        return call(
            body,
            [((size, chunk), F32)],
            [VMEM] * (2 + rows),
            [inverse, known] + list(parts),
            "backward_last",
            solve_flops,
        )[0]

    group = range(CHUNKS)
    field = [begin(i) for i in group]
    solved_t = [None] * CHUNKS
    for sweep in range(LEVELS - 1):
        for i in group:
            gathered = spread(field[i], "prow", rows)
            sums = forward_products(blocks, weights, gathered, rows, cols)
            parts = exchange(sums, "pcol", cols)
            if sweep < LEVELS - 2:
                field[i] = forward_solve(i, parts)
            else:
                field[i], solved_t[i] = forward_last(i, parts)
    top_answer = [None] * CHUNKS
    for i in group:
        gathered = spread(field[i], "prow", rows)
        sums = forward_products(links, link_weights, gathered, rows, cols)
        part = top_sum(exchange(sums, "pcol", cols))
        top_answer[i], field[i] = top_solve(i, spread(part, "layer", layers))
    known = [None] * CHUNKS
    for i in group:
        gathered = spread(field[i], "pcol", cols)
        sums = backward_products(links, link_weights, gathered, rows, cols)
        known[i], field[i] = backward_first(solved_t[i], exchange(sums, "prow", rows))
    for sweep in range(LEVELS - 1):
        for i in group:
            gathered = spread(field[i], "pcol", cols)
            sums = backward_products(blocks, weights, gathered, rows, cols)
            parts = exchange(sums, "prow", rows)
            finish = backward_solve if sweep < LEVELS - 2 else backward_last
            field[i] = finish(known[i], parts)
    answer = jnp.concatenate(field, axis=1)
    top = jnp.concatenate(top_answer, axis=1)
    return answer.reshape(rhs_sub.shape), top.reshape(rhs_top.shape)


def solution(mesh):
    blocked = P("layer", "prow", None, None, "pcol", None, None)
    scales = P("layer", "prow", None, None, "pcol")
    lower = P("layer", "prow", "pcol", None, None)
    upper = P("prow", "pcol", None, None)
    return jax.shard_map(
        shards,
        mesh=mesh,
        in_specs=(blocked, scales, scales, blocked, scales, scales, lower, upper, lower, upper),
        out_specs=(lower, upper),
        check_vma=False,
    )
```

```python
import jax
import jax.numpy as jnp
from jax import lax
from jax.experimental import pallas as pl
from jax.experimental.pallas import tpu as pltpu
from jax.sharding import PartitionSpec as P


LEVELS = 3
RELAYED = ("back1",)
HIGH_PREC = lax.Precision.HIGHEST
F32 = jnp.float32
BF16 = jnp.bfloat16

SMEM = pl.BlockSpec(memory_space=pltpu.SMEM)
VMEM = pl.BlockSpec(memory_space=pltpu.VMEM)
HBM = pl.BlockSpec(memory_space=pltpu.HBM)


def partner(index, step, count):
    if count & (count - 1) == 0:
        return index ^ step
    return (index + step) % count


def source(index, step, count):
    if count & (count - 1) == 0:
        return index ^ step
    return (index + count - step) % count


def send(value, axis, step, count):
    pairs = [(index, partner(index, step, count)) for index in range(count)]
    return lax.ppermute(value, axis, pairs)


def scatter_order(count):
    return range(1, count)


def gather_order(count):
    return reversed(range(1, count))


SMALL, LARGE = 16 * 1024 * 1024, 16 * 1024 * 1024


def call(body, outs, specs, operands, flops, scratch=()):
    size = sum(x.size * x.dtype.itemsize for x in operands)
    return pl.pallas_call(
        body,
        out_shape=[jax.ShapeDtypeStruct(shape, dtype) for shape, dtype in outs],
        in_specs=specs,
        out_specs=[VMEM] * len(outs),
        scratch_shapes=list(scratch),
        cost_estimate=pl.CostEstimate(flops=flops, bytes_accessed=size, transcendentals=0),
        compiler_params=pltpu.CompilerParams(vmem_limit_bytes=LARGE if HBM in specs else SMALL),
    )(*operands)


def gather(value, axis, count, name=""):
    received = [value] + [None] * (count - 1)
    if count == 4 and name in RELAYED:
        received[2] = send(value, axis, 2, count)
        received[1] = send(value, axis, 1, count)
        received[3] = send(received[2], axis, 1, count)
        return received
    for step in gather_order(count):
        received[step] = send(value, axis, step, count)
    return received


def add_pair(first, second):
    def body(first_ref, second_ref, out_ref):
        out_ref[...] = (first_ref[...].astype(F32) + second_ref[...].astype(F32)).astype(BF16)

    return call(body, [(first.shape, BF16)], [VMEM] * 2, [first, second], first.size)[0]


def scatter(values, axis, count, name=""):
    received = [values[0]] + [None] * (count - 1)
    if count == 4 and name in RELAYED:
        passed = send(values[3], axis, 1, count)
        received[1] = send(values[1], axis, 1, count)
        received[2] = send(add_pair(values[2], passed), axis, 2, count)
        return received[:3]
    for step in scatter_order(count):
        received[step] = send(values[step], axis, step, count)
    return received


def solve_dot(a, b):
    return jnp.dot(a, b, precision=HIGH_PREC, preferred_element_type=F32)


def total_of(refs):
    total = refs[0][...].astype(F32)
    for ref in refs[1:]:
        total = total + ref[...].astype(F32)
    return total


def products(blocks, weights, fields, axes, stacked=False, fetch=None):
    rows, cols = lax.axis_size("prow"), lax.axis_size("pcol")
    forward = axes == ("prow", "pcol")
    back_count, out_count = (rows, cols) if forward else (cols, rows)
    shape = fields[0].shape

    def body(weight_ref, blocks_ref, *refs):
        if fetch is not None:
            copy = pltpu.make_async_copy(refs[back_count], refs[-2], refs[-1])
            copy.start()
        ins = refs[:back_count]
        outs = refs[back_count + (fetch is not None) :]
        here_in, here_out = lax.axis_index(axes[0]), lax.axis_index(axes[1])
        for step in reversed(range(out_count)):
            target = partner(here_out, step, out_count)
            total = None
            for back in range(back_count):
                origin = source(here_in, back, back_count)
                block = target * rows + origin if forward else origin * rows + target
                if forward:
                    term = jnp.dot(blocks_ref[block], ins[back][...], preferred_element_type=F32)
                else:
                    term = jnp.dot(ins[back][...], blocks_ref[block], preferred_element_type=F32)
                term = term * weight_ref[block]
                total = term if total is None else total + term
            if stacked:
                outs[0][step] = total.astype(BF16)
            else:
                outs[step][...] = total.astype(BF16)
        if fetch is not None:
            copy.wait()

    if stacked:
        outs = [((out_count,) + shape, BF16)]
    else:
        outs = [(shape, BF16)] * out_count
    specs = [SMEM, VMEM] + [VMEM] * back_count
    operands = [weights, blocks] + list(fields)
    scratch = []
    if fetch is not None:
        specs.append(HBM)
        operands.append(fetch)
        outs.append((fetch.shape, fetch.dtype))
        scratch.append(pltpu.SemaphoreType.DMA)
    return call(
        body, outs, specs, operands, 2 * rows * cols * shape[0] * shape[1] * max(shape), scratch
    )


def load(blocks, after):
    def body(blocks_ref, after_ref, out_ref, sem):
        copy = pltpu.make_async_copy(blocks_ref, out_ref, sem)
        copy.start()
        copy.wait()

    return call(
        body,
        [(blocks.shape, blocks.dtype)],
        [HBM, VMEM],
        [blocks, after],
        0,
        [pltpu.SemaphoreType.DMA],
    )[0]


def weigh(scales, pattern, count):
    return (scales * pattern.astype(F32)).reshape(count)


def shards(
    factor,
    factor_scale,
    sub_pattern,
    coupling,
    coupling_scale,
    top_pattern,
    diag_inverse,
    top_inverse,
    rhs_sub,
    rhs_top,
):
    size = factor.shape[5]
    cols = factor.shape[2]
    rows = factor.shape[3]
    layers = lax.axis_size("layer")
    width = rhs_sub.shape[-1]
    chunk = width // layers
    blocks = factor.reshape(rows * cols, size, size)
    links = coupling.reshape(rows * cols, size, size)
    weights = weigh(factor_scale, sub_pattern, rows * cols)
    link_weights = weigh(coupling_scale, top_pattern, rows * cols)
    inverse = diag_inverse.reshape(size, size)
    top_matrix = top_inverse.reshape(size, size)
    own_rhs = rhs_sub.reshape(size, width)
    top_rhs = rhs_top.reshape(size, width)
    solve_flops = 12 * size * size * chunk
    tall, flat = (size, chunk), (chunk, size)

    def window(index):
        return slice(index * chunk, (index + 1) * chunk)

    def moving_window(index):
        return pl.ds(pl.multiple_of(index * chunk, chunk), chunk)

    def begin_loading():
        def body(inv_hbm, rhs_hbm, field_ref, inv_ref, rhs_ref, sems):
            copies = [
                pltpu.make_async_copy(inv_hbm, inv_ref, sems.at[0]),
                pltpu.make_async_copy(rhs_hbm, rhs_ref, sems.at[1]),
            ]
            for copy in copies:
                copy.start()
            for copy in copies:
                copy.wait()
            field_ref[...] = solve_dot(inv_ref[...], rhs_ref[:, window(0)]).astype(BF16)

        return call(
            body,
            [(tall, BF16), (inverse.shape, F32), (own_rhs.shape, F32)],
            [HBM] * 2,
            [inverse, own_rhs],
            solve_flops,
            [pltpu.SemaphoreType.DMA((2,))],
        )

    def begin(index):
        def body(inv_ref, rhs_ref, out_ref):
            out_ref[...] = solve_dot(inv_ref[...], rhs_ref[:, window(index)]).astype(BF16)

        return call(body, [(tall, BF16)], [VMEM] * 2, [inverse, own_rhs], solve_flops)[0]

    def forward_solve(index, parts, last):
        def body(inv_ref, rhs_ref, *refs):
            lower = total_of(refs[: len(parts)])
            outs = refs[len(parts) :]
            solved = solve_dot(inv_ref[...], rhs_ref[:, window(index)] - lower)
            outs[0][...] = solved.astype(BF16)
            if last:
                outs[1][...] = solved.T

        return call(
            body,
            [(tall, BF16)] + [(flat, F32)] * last,
            [VMEM] * (2 + len(parts)),
            [inverse, own_rhs] + list(parts),
            solve_flops,
        )

    def pick_other(stacks):
        def body(*refs):
            here = lax.axis_index("layer")
            for step in range(1, layers):
                for index in range(layers):

                    @pl.when(partner(here, step, layers) == index)
                    def _(step=step, index=index):
                        refs[layers + step - 1][...] = refs[index][...]

        return call(
            body,
            [(stacks[0].shape, BF16)] * (layers - 1),
            [VMEM] * layers,
            list(stacks),
            stacks[0].size,
        )

    def merge(stacks, others):
        def body(*refs):
            here = lax.axis_index("layer")
            outs = refs[2 * layers - 1 :]
            for index in range(layers):

                @pl.when(here == index)
                def _(index=index):
                    for step in range(cols):
                        total = refs[index][step].astype(F32)
                        for other in refs[layers : 2 * layers - 1]:
                            total = total + other[step].astype(F32)
                        outs[step][...] = total.astype(BF16)

        return call(
            body,
            [(tall, BF16)] * cols,
            [VMEM] * (2 * layers - 1),
            list(stacks) + list(others),
            stacks[0].size,
        )

    def top_solve(parts):
        def body(top_ref, rhs_ref, *refs):
            here = lax.axis_index("layer")
            merged = total_of(refs[: len(parts)])
            outs = refs[len(parts) :]
            half = solve_dot(top_ref[...], rhs_ref[:, moving_window(here)] - merged)
            answer = solve_dot(half.T, top_ref[...])
            outs[0][...] = answer
            outs[1][...] = answer.astype(BF16)

        return call(
            body,
            [(flat, F32), (flat, BF16)],
            [VMEM] * (2 + len(parts)),
            [top_matrix, top_rhs] + list(parts),
            2 * solve_flops,
        )

    def backward_first(slot, solved, parts):
        def body(inv_ref, *refs):
            here = lax.axis_index("layer")
            known_ref, out_ref = refs[-2:]
            coupled = total_of(refs[layers:-2])
            chosen = refs[0][...]
            for index in range(1, layers):
                chosen = jnp.where(partner(here, slot, layers) == index, refs[index][...], chosen)
            known = chosen - coupled
            known_ref[...] = known
            out_ref[...] = solve_dot(known, inv_ref[...]).astype(BF16)

        return call(
            body,
            [(flat, F32), (flat, BF16)],
            [VMEM] * (1 + layers + len(parts)),
            [inverse] + list(solved) + list(parts),
            solve_flops,
        )

    def backward_solve(known, parts):
        def body(inv_ref, known_ref, *refs):
            upper = total_of(refs[:-1])
            refs[-1][...] = solve_dot(known_ref[...] - upper, inv_ref[...]).astype(BF16)

        return call(
            body,
            [(flat, BF16)],
            [VMEM] * (2 + len(parts)),
            [inverse, known] + list(parts),
            solve_flops,
        )[0]

    def finish(known, parts, tops):
        terms = len(parts[0])

        def body(inv_ref, *refs):
            here = lax.axis_index("layer")
            out_ref, top_ref = refs[-2:]
            for slot in range(layers):
                window_ref = moving_window(partner(here, slot, layers))
                top_ref[:, window_ref] = refs[slot][...].T
                known_ref = refs[layers + slot]
                low = 2 * layers + slot * terms
                upper = total_of(refs[low : low + terms])
                answer = solve_dot(known_ref[...] - upper, inv_ref[...])
                out_ref[:, window_ref] = answer.T

        operands = [inverse] + list(tops) + list(known) + [x for group in parts for x in group]
        return call(
            body, [((size, width), F32)] * 2, [VMEM] * len(operands), operands, layers * solve_flops
        )

    group = range(layers)
    down, up = ("prow", "pcol"), ("pcol", "prow")
    first, inverse, own_rhs = begin_loading()
    field = [first] + [begin(i) for i in group if i]
    blocks = load(blocks, field[-1])
    solved = [None] * layers
    for sweep in range(LEVELS - 1):
        last = sweep == LEVELS - 2
        for i in group:
            gathered = gather(field[i], "prow", rows, f"forward{sweep}")
            if last and i == 0:
                *sums, links = products(blocks, weights, gathered, down, fetch=links)
            else:
                sums = products(blocks, weights, gathered, down)
            results = forward_solve(i, scatter(sums, "pcol", cols), last)
            field[i] = results[0]
            if last:
                solved[i] = results[1]
    stacks = []
    for i in group:
        stacks += products(
            links, link_weights, gather(field[i], "prow", rows, "links"), down, stacked=True
        )
    others = [
        send(value, "layer", step + 1, layers) for step, value in enumerate(pick_other(stacks))
    ]
    received = [None] * cols
    shares = merge(stacks, others)
    for step in reversed(range(cols)):
        received[step] = send(shares[step], "pcol", step, cols) if step else shares[0]
    top_own, top_field = top_solve(received)
    tops = [top_own] + [send(top_own, "layer", step, layers) for step in range(1, layers)]
    gathered = [None] * cols
    for step in reversed(range(cols)):
        gathered[step] = send(top_field, "pcol", step, cols) if step else top_field
    known, field = [None] * layers, [None] * layers
    for slot in group:
        values = gathered
        if slot:
            values = [send(value, "layer", slot, layers) for value in gathered]
        sums = products(links, link_weights, values, up)
        coupled = scatter(sums, "prow", rows, "couple")
        known[slot], field[slot] = backward_first(slot, solved, coupled)
    for sweep in range(LEVELS - 1):
        parts = [None] * layers
        for slot in group:
            sums = products(blocks, weights, gather(field[slot], "pcol", cols), up)
            parts[slot] = scatter(sums, "prow", rows, f"back{sweep}")
            if sweep < LEVELS - 2:
                field[slot] = backward_solve(known[slot], parts[slot])
    answer, top = finish(known, parts, tops)
    return answer.reshape(rhs_sub.shape), top.reshape(rhs_top.shape)


def solution(mesh):
    blocked = P("layer", "prow", None, None, "pcol", None, None)
    scales = P("layer", "prow", None, None, "pcol")
    lower = P("layer", "prow", "pcol", None, None)
    upper = P("prow", "pcol", None, None)
    return jax.shard_map(
        shards,
        mesh=mesh,
        in_specs=(blocked, scales, scales, blocked, scales, scales, lower, upper, lower, upper),
        out_specs=(lower, upper),
        check_vma=False,
    )
```
